32 devices in a mesh: groups: 2 (over x), seq: 16 (over z, y, core).
Axes of the slice: x: 2, y: 2, z: 4, core: 2. Of those that a mesh axis runs over, the one named last changes fastest.
Arguments:
- sequence: bfloat16 [8192, 1536], P(('groups', 'seq')), parts along dimension 0, may hold values from -6 to 6
- gain_conv: float32 [1536], replicated, may hold values from 0.25 to 1.75
- conv_weight: float32 [5, 1536], replicated, may hold values from -3 to 3
- gain_attn: float32 [1536], replicated, may hold values from 0.25 to 1.75
- w_query: bfloat16 [1536, 1024], replicated
- w_key: bfloat16 [1536, 128], replicated
- w_value: bfloat16 [1536, 192], replicated, may hold values from -0.15625 to 0.15625
- w_out: bfloat16 [1536, 1536], replicated, may hold values from -0.15625 to 0.15625
- w_left: bfloat16 [1536, 128], replicated, may hold values from -0.15625 to 0.15625
- w_right: bfloat16 [1536, 128], replicated, may hold values from -0.15625 to 0.15625
- w_pair: bfloat16 [3, 3, 128, 128], replicated, may hold values from -0.1875 to 0.1875
Outputs:
- track: bfloat16 [8192, 1536], P(('groups', 'seq')), parts along dimension 0
- pair_map: bfloat16 [512, 256, 128], P(('groups', 'seq')), parts along dimension 0
The draws below stay inside these ranges and needn't reach their ends.
There are 2 independent parts, one for each index of `groups`. The reference program is written for one: setup_inputs(seed, part) draws one part's arguments, and reference() takes and returns one part's arrays. A program takes and returns all parts, laid end to end along the dimension named above; an argument that names none is the same for every part. Nothing has to cross between parts.
All inputs are finite; a program needn't handle non-finite values.
Results may differ from the reference program's by a relative error of at most 0.019.
Values may be sent and summed in bfloat16 or wider, within the bound.
A program may use at most 128 MiB of HBM per device.

```python
import jax
import jax.numpy as jnp
from jax import lax

D = 1536
HEADS = 8
KEY = 128
VAL = 192
PAIR = 128
POOL = 16
CONV = 5
SEQ = 4096
PROWS = 256


def shared_keys(key):
    return jax.random.normal(jax.random.fold_in(key, 11), (D, KEY), jnp.float32) * D ** (-0.5)


def draw_w_key(key, part):
    return shared_keys(key).astype(jnp.bfloat16)


def turned_keys(key):
    base = shared_keys(key)
    flips = jax.random.bernoulli(jax.random.fold_in(key, 31), 0.5, (HEADS, KEY)).astype(jnp.float32) * 2.0 - 1.0
    turned = [jnp.roll(base, 1 + head, axis=1) * flips[head][None, :] for head in range(HEADS)]
    return jnp.stack(turned, axis=1)


def draw_w_query(key, part):
    own = jax.random.normal(jax.random.fold_in(key, 23), (D, HEADS, KEY), jnp.float32) * D ** (-0.5)
    strength = jax.random.uniform(jax.random.fold_in(key, 37), (HEADS,), jnp.float32, 1.5, 2.6)
    coupled = strength[None, :, None] * turned_keys(key) + 0.3 * own
    return coupled.reshape(D, HEADS * KEY).astype(jnp.bfloat16)


def steps_of(key, shape, pieces, low, largest):
    def one(dim, blocks):
        steps = jax.random.uniform(jax.random.fold_in(jax.random.fold_in(key, 6), dim), (blocks,), jnp.float32, low / len(pieces), largest / len(pieces))
        return jnp.repeat(jnp.exp(steps), shape[dim] // blocks).reshape((-1,) + (1,) * (len(shape) - dim - 1))

    level = one(*pieces[0])
    for cut in pieces[1:]:
        level = level * one(*cut)
    return level


def gaussian(rng, shape, scale, reach, cuts=(), kind=jnp.bfloat16):
    level = steps_of(rng, shape, cuts, -0.22, 0.18) if cuts else 1.0
    values = jax.random.normal(rng, shape, jnp.float32) * scale * level
    return jnp.minimum(jnp.maximum(values, -reach), reach).astype(kind)


def setup_inputs(seed: int = 0, part: int = 0) -> dict:
    key_of = jax.random.split(jax.random.key(seed), 12)
    own_keys = jax.random.split(jax.random.fold_in(key_of[11], part), 12)
    return {
        "sequence": gaussian(own_keys[0], (SEQ, D), 1.0, 6.0, ((0, 16),)),
        "gain_conv": jnp.clip(1.0 + 0.15 * jax.random.normal(key_of[1], (D,), jnp.float32), 0.25, 1.75),
        "conv_weight": gaussian(key_of[2], (CONV, D), 0.5, 3.0, (), jnp.float32),
        "gain_attn": jnp.clip(1.0 + 0.15 * jax.random.normal(key_of[3], (D,), jnp.float32), 0.25, 1.75),
        "w_query": draw_w_query(jax.random.fold_in(key_of[11], 71), part),
        "w_key": draw_w_key(jax.random.fold_in(key_of[11], 71), part),
        "w_value": gaussian(key_of[6], (D, VAL), D ** -0.5, 0.15625),
        "w_out": gaussian(key_of[7], (HEADS * VAL, D), (HEADS * VAL) ** -0.5, 0.15625),
        "w_left": gaussian(key_of[8], (D, PAIR), D ** -0.5, 0.15625),
        "w_right": gaussian(key_of[9], (D, PAIR), D ** -0.5, 0.15625),
        "w_pair": gaussian(key_of[10], (3, 3, PAIR, PAIR), (9 * PAIR) ** -0.5, 0.1875),
    }


def rms_norm(values, gain):
    values = values.astype(jnp.float32)
    scale = lax.rsqrt(lax.optimization_barrier(jnp.mean(values * values, axis=-1, keepdims=True)) + 1e-06)
    return values * scale * gain

def reference(sequence, gain_conv, conv_weight, gain_attn, w_query, w_key, w_value, w_out, w_left, w_right, w_pair):
    normed = rms_norm(sequence, gain_conv).astype(jnp.bfloat16)
    padded = jnp.pad(normed.astype(jnp.float32), ((2, 2), (0, 0)))
    convolved = jnp.zeros((SEQ, D), jnp.float32)
    for offset in range(CONV):
        convolved = convolved + conv_weight[offset][None, :] * padded[offset:offset + SEQ]
    first = (sequence.astype(jnp.float32) + convolved).astype(jnp.bfloat16)
    attn_in = rms_norm(first, gain_attn).astype(jnp.bfloat16)
    queries = jnp.dot(attn_in, w_query, preferred_element_type=jnp.float32).astype(jnp.bfloat16)
    keys = jnp.dot(attn_in, w_key, preferred_element_type=jnp.float32).astype(jnp.bfloat16).astype(jnp.float32)
    values = jnp.dot(attn_in, w_value, preferred_element_type=jnp.float32).astype(jnp.bfloat16).astype(jnp.float32)
    block = min(512, SEQ)
    query_blocks = queries.reshape(SEQ // block, block, HEADS, KEY)
    scale = 1.0 / jnp.sqrt(jnp.float32(KEY))

    def attend(query_block):
        scores = jnp.einsum('qhd,kd->hqk', query_block.astype(jnp.float32), keys) * scale
        top = lax.optimization_barrier(jnp.max(scores, axis=-1, keepdims=True))
        expo = jnp.exp(scores - top)
        total = lax.optimization_barrier(jnp.sum(expo, axis=-1))
        rounded = expo.astype(jnp.bfloat16).astype(jnp.float32)
        numer = jnp.einsum('hqk,kv->hqv', rounded, values)
        result = numer / total[..., None]
        return jnp.transpose(result, (1, 0, 2)).reshape(block, HEADS * VAL).astype(jnp.bfloat16)
    attended = lax.map(attend, query_blocks).reshape(SEQ, HEADS * VAL)
    track = (first.astype(jnp.float32) + jnp.dot(attended, w_out, preferred_element_type=jnp.float32)).astype(jnp.bfloat16)
    pooled = lax.optimization_barrier(jnp.mean(track.astype(jnp.float32).reshape(PROWS, POOL, D), axis=1)).astype(jnp.bfloat16)
    left = jnp.dot(pooled, w_left, preferred_element_type=jnp.float32).astype(jnp.bfloat16)
    right = jnp.dot(pooled, w_right, preferred_element_type=jnp.float32).astype(jnp.bfloat16)
    pair0 = (left.astype(jnp.float32)[:, None, :] * right.astype(jnp.float32)[None, :, :]).astype(jnp.bfloat16)
    activated = jax.nn.gelu(pair0.astype(jnp.float32)).astype(jnp.bfloat16)
    grid = jnp.pad(activated, ((1, 1), (1, 1), (0, 0)))
    summed = jnp.zeros((PROWS * PROWS, PAIR), jnp.float32)
    for row_off in range(3):
        for col_off in range(3):
            window = grid[row_off:row_off + PROWS, col_off:col_off + PROWS].reshape(PROWS * PROWS, PAIR)
            summed = summed + jnp.dot(window, w_pair[row_off, col_off], preferred_element_type=jnp.float32)
    pair_map = (pair0.astype(jnp.float32) + summed.reshape(PROWS, PROWS, PAIR)).astype(jnp.bfloat16)
    return (track, pair_map)
```

```python
import functools
import math

import jax
import jax.numpy as jnp
from jax import lax
from jax.experimental import pallas as pl
from jax.experimental.pallas import tpu as pltpu
from jax.sharding import PartitionSpec as P

HEADS = 8
POOL = 16
HALO = 16
PARTS = 2
F32 = jnp.float32
BF16 = jnp.bfloat16


def dot(a, b):
    return jnp.dot(a, b, preferred_element_type=F32)


def dot_t(a, b):
    return lax.dot_general(a, b, (((1,), (1,)), ((), ())), preferred_element_type=F32)


def rms_norm(values, gain):
    scale = lax.rsqrt(jnp.mean(values * values, axis=-1, keepdims=True) + 1e-06)
    return values * scale * gain


def kernel(
    n,
    seq_ref, gconv_ref, conv_ref, gattn_ref,
    wq_hbm, wk_hbm, wv_hbm, wo_hbm, wl_hbm, wr_hbm, wp_hbm,
    track_ref, pair_ref,
    wq, wk, wv, wo, wl, wr, wp,
    halo, padded, first, attn, q_ref, kv, acc, top, attended,
    own_left, left_halo, left_ext, right_land, right_all, act,
    w_sem, halo_send, halo_recv, r_send, l_send, p_send, kv_recv,
    left_send, left_recv, right_send, right_recv,
):
    rows, width = seq_ref.shape
    key = wk.shape[1]
    val = wv.shape[1]
    taps = conv_ref.shape[0]
    reach = taps // 2
    part = rows // PARTS
    chips = n // 2
    half = (chips + 1) // 2
    me = lax.axis_index("seq")
    chip = me // 2
    core = me % 2
    partner = chip * 2 + (1 - core)
    pos = jnp.where(chip % 2 == 0, chip // 2, chips - 1 - chip // 2)

    def chip_at(place):
        place = lax.rem(place + 2 * chips, chips)
        return jnp.where(place < half, 2 * place, 2 * (chips - 1 - place) + 1)

    def mine_at(place):
        return chip_at(place) * 2 + core

    def other_at(place):
        return chip_at(place) * 2 + (1 - core)

    barrier = pltpu.get_barrier_semaphore()

    @pl.loop(1, n)
    def _(step):
        pl.semaphore_signal(barrier, inc=1, device_id={"seq": lax.rem(me + step, n)})

    pairs = ((wk_hbm, wk), (wv_hbm, wv), (wq_hbm, wq), (wo_hbm, wo), (wl_hbm, wl), (wr_hbm, wr), (wp_hbm, wp))
    loads = [pltpu.make_async_copy(s, d, w_sem.at[i]) for i, (s, d) in enumerate(pairs)]
    for load in loads:
        load.start()
    pl.semaphore_wait(barrier, n - 1)

    def send(src, dst, ssem, rsem, to):
        return pltpu.make_async_remote_copy(
            src_ref=src, dst_ref=dst, send_sem=ssem, recv_sem=rsem, device_id={"seq": to}
        )

    has_prev = me > 0
    has_next = me < n - 1
    prev = lax.rem(me + n - 1, n)
    after = lax.rem(me + 1, n)
    to_next = send(seq_ref.at[pl.ds(rows - HALO, HALO)], halo.at[0], halo_send.at[0], halo_recv.at[0], after)
    to_prev = send(seq_ref.at[pl.ds(0, HALO)], halo.at[1], halo_send.at[1], halo_recv.at[1], prev)

    @pl.when(has_next)
    def _():
        to_next.start()

    @pl.when(has_prev)
    def _():
        to_prev.start()

    gconv = gconv_ref[...]
    strip = 32
    for start in range(0, rows, strip):
        values = seq_ref[start:start + strip, :].astype(F32)
        padded[HALO + start:HALO + start + strip, :] = rms_norm(values, gconv).astype(BF16).astype(F32)

    @pl.when(has_prev)
    def _():
        to_next.wait_recv()
        padded[0:HALO, :] = rms_norm(halo[0].astype(F32), gconv).astype(BF16).astype(F32)

    @pl.when(jnp.logical_not(has_prev))
    def _():
        padded[0:HALO, :] = jnp.zeros((HALO, width), F32)

    @pl.when(has_next)
    def _():
        to_prev.wait_recv()
        padded[HALO + rows:, :] = rms_norm(halo[1].astype(F32), gconv).astype(BF16).astype(F32)

    @pl.when(jnp.logical_not(has_next))
    def _():
        padded[HALO + rows:, :] = jnp.zeros((HALO, width), F32)

    gattn = gattn_ref[...]
    for start in range(0, rows, strip):
        total = seq_ref[start:start + strip, :].astype(F32)
        conv = jnp.zeros((strip, width), F32)
        for tap in range(taps):
            base = HALO + start + tap - reach
            conv = conv + conv_ref[tap:tap + 1, :] * padded[base:base + strip, :]
        one = (total + conv).astype(BF16)
        first[start:start + strip, :] = one
        attn[start:start + strip, :] = rms_norm(one.astype(F32), gattn).astype(BF16)

    loads[0].wait()
    loads[1].wait()
    kv[me, :, 0:key] = dot(attn[...], wk[...]).astype(BF16)
    kv[me, :, key:key + val] = dot(attn[...], wv[...]).astype(BF16)
    kv[me, :, key + val:] = jnp.ones((rows, kv.shape[2] - key - val), BF16)

    right_steps = chips // 2
    left_steps = chips - 1 - right_steps
    to_right = mine_at(pos + 1)
    to_left = mine_at(pos - 1)

    def piece(slot, c):
        return kv.at[slot, pl.ds(c * part, part)]

    def copy_right(t, c):
        slot = mine_at(pos - t)
        return send(piece(slot, c), piece(slot, c), r_send.at[t, c], kv_recv.at[slot, c], to_right)

    def copy_left(t, c):
        slot = mine_at(pos + t)
        return send(piece(slot, c), piece(slot, c), l_send.at[t, c], kv_recv.at[slot, c], to_left)

    def copy_partner(slot, count, c):
        return send(piece(slot, c), piece(slot, c), p_send.at[count, c], kv_recv.at[slot, c], partner)

    def arrived(slot, c):
        send(piece(slot, c), piece(slot, c), p_send.at[0, c], kv_recv.at[slot, c], partner).wait_recv()

    sent = []

    def go(copy):
        copy.start()
        sent.append(copy)

    for c in range(PARTS):
        if right_steps:
            go(copy_right(0, c))
        if left_steps:
            go(copy_left(0, c))
        go(copy_partner(me, 0, c))

    loads[2].wait()
    scale = math.log2(math.e) / math.sqrt(key)
    for h in range(HEADS):
        q_ref[h] = (dot(attn[...], wq[:, h * key:(h + 1) * key]) * scale).astype(BF16)

    def attend(pieces, initial):
        keys = jnp.concatenate([kv[s, c * part:(c + 1) * part, 0:key] for s, c in pieces], axis=0)
        values = jnp.concatenate([kv[s, c * part:(c + 1) * part, key:] for s, c in pieces], axis=0)
        wide = keys.shape[0] // 128

        @pl.loop(0, HEADS, unroll=2)
        def _(h):
            scores = dot_t(q_ref[h], keys)
            best = jnp.broadcast_to(jnp.max(scores, axis=1, keepdims=True), (rows, 128))
            if not initial:
                old = top[h]
                best = jnp.maximum(old, best)
            weights = jnp.exp2(scores - jnp.concatenate([best] * wide, axis=1)).astype(BF16)
            update = dot(weights, values)
            if initial:
                acc[h] = update
            else:
                factor = jnp.exp2(old - best)
                acc[h] = acc[h] * jnp.concatenate([factor] * (update.shape[1] // 128), axis=1) + update
            top[h] = best

    for c in range(PARTS):
        arrived(partner, c)
    attend([(s, c) for s in (me, partner) for c in range(PARTS)], True)

    waiting = None
    count = 1
    for t in range(right_steps):
        both = t < left_steps
        slots = [pos - 1 - t] + ([pos + 1 + t] if both else [])
        for c in range(PARTS):
            for k, place in enumerate(slots):
                slot = mine_at(place)
                arrived(slot, c)
                if k == 0 and t + 1 < right_steps:
                    go(copy_right(t + 1, c))
                if k == 1 and t + 1 < left_steps:
                    go(copy_left(t + 1, c))
                go(copy_partner(slot, count + k, c))
            if waiting is not None:
                for s, cc in waiting[1]:
                    arrived(s, cc)
                attend(waiting[0] + waiting[1], False)
            waiting = ([(mine_at(p), c) for p in slots], [(other_at(p), c) for p in slots])
        count += len(slots)
    if waiting is not None:
        for s, cc in waiting[1]:
            arrived(s, cc)
        attend(waiting[0] + waiting[1], False)

    for pair in range(0, HEADS, 2):
        both = []
        for h in (pair, pair + 1):
            block = acc[h]
            both.append((block[:, :val] / block[:, val:val + 1]).astype(BF16))
        attended[:, pair * val:(pair + 2) * val] = jnp.concatenate(both, axis=1)

    loads[3].wait()
    band = rows // POOL
    member = lax.broadcasted_iota(jnp.int32, (band, rows), 1) // POOL
    pool = jnp.where(member == lax.broadcasted_iota(jnp.int32, (band, rows), 0), 1.0 / POOL, 0.0).astype(BF16)
    loads[4].wait()
    loads[5].wait()
    left = jnp.zeros((band, wl.shape[1]), F32)
    right = jnp.zeros((band, wr.shape[1]), F32)
    cols = 512 if width % 512 == 0 else width
    for start in range(0, width, cols):
        stop = start + cols
        block = (first[:, start:stop].astype(F32) + dot(attended[...], wo[:, start:stop])).astype(BF16)
        track_ref[:, start:stop] = block
        pooled = dot(pool, block).astype(BF16)
        left = left + dot(pooled, wl[start:stop, :])
        right = right + dot(pooled, wr[start:stop, :])
    own_left[...] = left.astype(BF16)
    right_land[me] = right.astype(BF16)

    left_next = send(own_left, left_halo.at[0], left_send.at[0], left_recv.at[0], after)
    left_prev = send(own_left, left_halo.at[1], left_send.at[1], left_recv.at[1], prev)

    @pl.when(has_next)
    def _():
        left_next.start()

    @pl.when(has_prev)
    def _():
        left_prev.start()

    def right_copy(step):
        return send(right_land.at[me], right_land.at[me], right_send.at[step], right_recv.at[me], lax.rem(me + step, n))

    @pl.loop(1, n)
    def _(step):
        right_copy(step).start()

    left_ext[...] = jnp.zeros(left_ext.shape, F32)
    left_ext[8:8 + band, :] = own_left[...].astype(F32)

    @pl.when(has_prev)
    def _():
        left_next.wait_recv()
        left_ext[7:8, :] = left_halo[0].astype(F32)[band - 1:band, :]

    @pl.when(has_next)
    def _():
        left_prev.wait_recv()
        left_ext[8 + band:9 + band, :] = left_halo[1].astype(F32)[0:1, :]

    @pl.loop(1, n)
    def _(step):
        slot = lax.rem(me + step, n)
        send(right_land.at[slot], right_land.at[slot], right_send.at[step], right_recv.at[slot], slot).wait_recv()

    columns = n * band
    right_all[...] = right_land[...].astype(F32).reshape(columns, right_all.shape[1])
    loads[6].wait()
    channels = right_all.shape[1]
    column = lax.broadcasted_iota(jnp.int32, (columns, channels), 0)

    @pl.loop(0, band + 2)
    def _(i):
        product = (left_ext[pl.ds(i + 7, 1), :] * right_all[...]).astype(BF16).astype(F32)
        active = jax.nn.gelu(product)
        act[i, :, 0:channels] = jnp.where(column == 0, 0.0, pltpu.roll(active, 1, 0)).astype(BF16)
        act[i, :, channels:2 * channels] = active.astype(BF16)
        act[i, :, 2 * channels:] = jnp.where(column == columns - 1, 0.0, pltpu.roll(active, columns - 1, 0)).astype(BF16)

    span = 3 * channels

    @pl.loop(0, band)
    def _(i):
        total = (left_ext[pl.ds(i + 8, 1), :] * right_all[...]).astype(BF16).astype(F32)
        for a in range(3):
            total = total + dot(act[i + a], wp[a * span:(a + 1) * span, :])
        pair_ref[i] = total.astype(BF16)

    @pl.when(has_next)
    def _():
        to_next.wait_send()
        left_next.wait_send()

    @pl.when(has_prev)
    def _():
        to_prev.wait_send()
        left_prev.wait_send()

    for copy in sent:
        copy.wait_send()

    @pl.loop(1, n)
    def _(step):
        right_copy(step).wait_send()


def solution(mesh):
    n = mesh.shape["seq"]

    def local(sequence, gain_conv, conv_weight, gain_attn, w_query, w_key, w_value, w_out, w_left, w_right, w_pair):
        rows, width = sequence.shape
        key, val = w_key.shape[1], w_value.shape[1]
        channels = w_left.shape[1]
        band = rows // POOL
        columns = n * band
        chips = n // 2
        value_lanes = (val // 128 + 1) * 128
        taps = w_pair.reshape(-1, channels)
        weights = (w_query, w_key, w_value, w_out, w_left, w_right, taps)
        vmem = pl.BlockSpec(memory_space=pltpu.VMEM)
        dma = pltpu.SemaphoreType.DMA
        steps = max(chips // 2, 1)
        return pl.pallas_call(
            functools.partial(kernel, n),
            out_shape=(
                jax.ShapeDtypeStruct((rows, width), BF16),
                jax.ShapeDtypeStruct((band, columns, channels), BF16),
            ),
            in_specs=[vmem] * 4 + [pl.BlockSpec(memory_space=pl.ANY)] * 7,
            out_specs=(vmem, vmem),
            scratch_shapes=[pltpu.VMEM(w.shape, BF16) for w in weights]
            + [
                pltpu.VMEM((2, HALO, width), BF16),
                pltpu.VMEM((rows + 2 * HALO, width), F32),
                pltpu.VMEM((rows, width), BF16),
                pltpu.VMEM((rows, width), BF16),
                pltpu.VMEM((HEADS, rows, key), BF16),
                pltpu.VMEM((n, rows, key + value_lanes), BF16),
                pltpu.VMEM((HEADS, rows, value_lanes), F32),
                pltpu.VMEM((HEADS, rows, 128), F32),
                pltpu.VMEM((rows, HEADS * val), BF16),
                pltpu.VMEM((band, channels), BF16),
                pltpu.VMEM((2, band, channels), BF16),
                pltpu.VMEM((band + 16, channels), F32),
                pltpu.VMEM((n, band, channels), BF16),
                pltpu.VMEM((columns, channels), F32),
                pltpu.VMEM((band + 2, columns, 3 * channels), BF16),
                dma((len(weights),)),
                dma((2,)),
                dma((2,)),
                dma((steps, PARTS)),
                dma((steps, PARTS)),
                dma((chips, PARTS)),
                dma((n, PARTS)),
                dma((2,)),
                dma((2,)),
                dma((n,)),
                dma((n,)),
            ],
            compiler_params=pltpu.CompilerParams(
                collective_id=0, has_side_effects=True, vmem_limit_bytes=60 * 1024 * 1024
            ),
        )(sequence, gain_conv.reshape(1, -1), conv_weight, gain_attn.reshape(1, -1), *weights)

    placed = (P(("groups", "seq"), None),) + (P(),) * 10
    return jax.shard_map(
        local,
        mesh=mesh,
        in_specs=placed,
        out_specs=(P(("groups", "seq"), None), P(("groups", "seq"), None, None)),
        check_vma=False,
    )
```

```python
import functools
import math

import jax
import jax.numpy as jnp
from jax import lax
from jax.experimental import pallas as pl
from jax.experimental.pallas import tpu as pltpu
from jax.sharding import PartitionSpec as P

HEADS = 8
POOL = 16
HALO = 16
PARTS = 2
F32 = jnp.float32
BF16 = jnp.bfloat16


def dot(a, b):
    return jnp.dot(a, b, preferred_element_type=F32)


def dot_t(a, b):
    return lax.dot_general(a, b, (((1,), (1,)), ((), ())), preferred_element_type=F32)


def rms_norm(values, gain):
    scale = lax.rsqrt(jnp.mean(values * values, axis=-1, keepdims=True) + 1e-06)
    return values * scale * gain


def kernel(
    n,
    seq_ref, conv_ref,
    gconv_hbm, gattn_hbm, wq_hbm, wk_hbm, wv_hbm, wo_hbm, wl_hbm, wr_hbm,
    track_hbm, left_ext, right_land,
    gains, wq, wk, wv, wo, wl, wr, track_ref,
    halo, padded, first, attn, q_ref, kv, acc, top, attended,
    own_left, left_halo,
    w_sem, track_sem, halo_send, halo_recv, r_send, l_send, p_send, kv_recv,
    left_send, left_recv, right_send, right_recv,
):
    rows, width = seq_ref.shape
    key = wk.shape[1]
    val = wv.shape[0]
    taps = conv_ref.shape[0]
    reach = taps // 2
    part = rows // PARTS
    chips = n // 2
    half = (chips + 1) // 2
    me = lax.axis_index("seq")
    chip = me // 2
    core = me % 2
    partner = chip * 2 + (1 - core)
    pos = jnp.where(chip % 2 == 0, chip // 2, chips - 1 - chip // 2)

    def chip_at(place):
        place = lax.rem(place + 2 * chips, chips)
        return jnp.where(place < half, 2 * place, 2 * (chips - 1 - place) + 1)

    def mine_at(place):
        return chip_at(place) * 2 + core

    def other_at(place):
        return chip_at(place) * 2 + (1 - core)

    barrier = pltpu.get_barrier_semaphore()

    @pl.loop(1, n)
    def _(step):
        pl.semaphore_signal(barrier, inc=1, device_id={"seq": lax.rem(me + step, n)})

    pairs = (
        (wk_hbm, wk), (wv_hbm, wv), (wq_hbm, wq), (wo_hbm, wo), (wl_hbm, wl), (wr_hbm, wr),
        (gconv_hbm, gains.at[0]), (gattn_hbm, gains.at[1]),
    )
    loads = [pltpu.make_async_copy(s, d, w_sem.at[i]) for i, (s, d) in enumerate(pairs)]
    for load in loads[6:] + loads[:6]:
        load.start()
    pl.semaphore_wait(barrier, n - 1)

    def send(src, dst, ssem, rsem, to):
        return pltpu.make_async_remote_copy(
            src_ref=src, dst_ref=dst, send_sem=ssem, recv_sem=rsem, device_id={"seq": to}
        )

    has_prev = me > 0
    has_next = me < n - 1
    prev = lax.rem(me + n - 1, n)
    after = lax.rem(me + 1, n)
    to_next = send(seq_ref.at[pl.ds(rows - HALO, HALO)], halo.at[0], halo_send.at[0], halo_recv.at[0], after)
    to_prev = send(seq_ref.at[pl.ds(0, HALO)], halo.at[1], halo_send.at[1], halo_recv.at[1], prev)

    @pl.when(has_next)
    def _():
        to_next.start()

    @pl.when(has_prev)
    def _():
        to_prev.start()

    loads[6].wait()
    loads[7].wait()
    gconv = gains[0:1, :]
    strip = 32
    for start in range(0, rows, strip):
        values = seq_ref[start:start + strip, :].astype(F32)
        padded[HALO + start:HALO + start + strip, :] = rms_norm(values, gconv).astype(BF16).astype(F32)

    @pl.when(has_prev)
    def _():
        to_next.wait_recv()
        padded[0:HALO, :] = rms_norm(halo[0].astype(F32), gconv).astype(BF16).astype(F32)

    @pl.when(jnp.logical_not(has_prev))
    def _():
        padded[0:HALO, :] = jnp.zeros((HALO, width), F32)

    @pl.when(has_next)
    def _():
        to_prev.wait_recv()
        padded[HALO + rows:, :] = rms_norm(halo[1].astype(F32), gconv).astype(BF16).astype(F32)

    @pl.when(jnp.logical_not(has_next))
    def _():
        padded[HALO + rows:, :] = jnp.zeros((HALO, width), F32)

    gattn = gains[1:2, :]
    for start in range(0, rows, strip):
        total = seq_ref[start:start + strip, :].astype(F32)
        conv = jnp.zeros((strip, width), F32)
        for tap in range(taps):
            base = HALO + start + tap - reach
            conv = conv + conv_ref[tap:tap + 1, :] * padded[base:base + strip, :]
        one = (total + conv).astype(BF16)
        first[start:start + strip, :] = one
        attn[start:start + strip, :] = rms_norm(one.astype(F32), gattn).astype(BF16)

    loads[0].wait()
    loads[1].wait()
    kv[me, :, 0:key] = dot(attn[...], wk[...]).astype(BF16)
    kv[me, :, key:key + val] = dot_t(attn[...], wv[...]).astype(BF16)
    kv[me, :, key + val:] = jnp.ones((rows, kv.shape[2] - key - val), BF16)

    right_steps = chips // 2
    left_steps = chips - 1 - right_steps
    to_right = mine_at(pos + 1)
    to_left = mine_at(pos - 1)

    def piece(slot, c):
        return kv.at[slot, pl.ds(c * part, part)]

    def copy_right(t, c):
        slot = mine_at(pos - t)
        return send(piece(slot, c), piece(slot, c), r_send.at[t, c], kv_recv.at[slot, c], to_right)

    def copy_left(t, c):
        slot = mine_at(pos + t)
        return send(piece(slot, c), piece(slot, c), l_send.at[t, c], kv_recv.at[slot, c], to_left)

    def copy_partner(slot, count, c):
        return send(piece(slot, c), piece(slot, c), p_send.at[count, c], kv_recv.at[slot, c], partner)

    def arrived(slot, c):
        send(piece(slot, c), piece(slot, c), p_send.at[0, c], kv_recv.at[slot, c], partner).wait_recv()

    sent = []

    def go(copy):
        copy.start()
        sent.append(copy)

    for c in range(PARTS):
        if right_steps:
            go(copy_right(0, c))
        if left_steps:
            go(copy_left(0, c))
        go(copy_partner(me, 0, c))

    loads[2].wait()
    scale = math.log2(math.e) / math.sqrt(key)
    for h in range(HEADS):
        q_ref[h] = (dot(attn[...], wq[:, h * key:(h + 1) * key]) * scale).astype(BF16)

    def attend(pieces, initial):
        keys = jnp.concatenate([kv[s, c * part:(c + 1) * part, 0:key] for s, c in pieces], axis=0)
        values = jnp.concatenate([kv[s, c * part:(c + 1) * part, key:] for s, c in pieces], axis=0)
        wide = keys.shape[0] // 128

        @pl.loop(0, HEADS, unroll=2)
        def _(h):
            scores = dot_t(q_ref[h], keys)
            best = jnp.broadcast_to(jnp.max(scores, axis=1, keepdims=True), (rows, 128))
            if not initial:
                old = top[h]
                best = jnp.maximum(old, best)
            weights = jnp.exp2(scores - jnp.concatenate([best] * wide, axis=1)).astype(BF16)
            update = dot(weights, values)
            if initial:
                acc[h] = update
            else:
                factor = jnp.exp2(old - best)
                acc[h] = acc[h] * jnp.concatenate([factor] * (update.shape[1] // 128), axis=1) + update
            top[h] = best

    for c in range(PARTS):
        arrived(partner, c)
    attend([(s, c) for s in (me, partner) for c in range(PARTS)], True)

    waiting = None
    count = 1
    for t in range(right_steps):
        both = t < left_steps
        slots = [pos - 1 - t] + ([pos + 1 + t] if both else [])
        for c in range(PARTS):
            for k, place in enumerate(slots):
                slot = mine_at(place)
                arrived(slot, c)
                if k == 0 and t + 1 < right_steps:
                    go(copy_right(t + 1, c))
                if k == 1 and t + 1 < left_steps:
                    go(copy_left(t + 1, c))
                go(copy_partner(slot, count + k, c))
            if waiting is not None:
                for s, cc in waiting[1]:
                    arrived(s, cc)
                attend(waiting[0] + waiting[1], False)
            waiting = ([(mine_at(p), c) for p in slots], [(other_at(p), c) for p in slots])
        count += len(slots)
    if waiting is not None:
        for s, cc in waiting[1]:
            arrived(s, cc)
        attend(waiting[0] + waiting[1], False)

    for pair in range(0, HEADS, 2):
        both = []
        for h in (pair, pair + 1):
            block = acc[h]
            both.append((block[:, :val] / block[:, val:val + 1]).astype(BF16))
        attended[:, pair * val:(pair + 2) * val] = jnp.concatenate(both, axis=1)

    loads[3].wait()
    band = rows // POOL
    member = lax.broadcasted_iota(jnp.int32, (band, rows), 1) // POOL
    pool = jnp.where(member == lax.broadcasted_iota(jnp.int32, (band, rows), 0), 1.0 / POOL, 0.0).astype(BF16)
    loads[4].wait()
    loads[5].wait()
    left = jnp.zeros((band, wl.shape[1]), F32)
    right = jnp.zeros((band, wr.shape[1]), F32)
    cols = 512 if width % 512 == 0 else width
    for start in range(0, width, cols):
        stop = start + cols
        block = (first[:, start:stop].astype(F32) + dot(attended[...], wo[:, start:stop])).astype(BF16)
        track_ref[:, start:stop] = block
        pooled = dot(pool, block).astype(BF16)
        left = left + dot(pooled, wl[start:stop, :])
        right = right + dot(pooled, wr[start:stop, :])
    track_out = pltpu.make_async_copy(track_ref, track_hbm, track_sem)
    track_out.start()
    own_left[...] = left.astype(BF16)
    right_land[me] = right.astype(BF16)

    left_next = send(own_left, left_halo.at[0], left_send.at[0], left_recv.at[0], after)
    left_prev = send(own_left, left_halo.at[1], left_send.at[1], left_recv.at[1], prev)

    @pl.when(has_next)
    def _():
        left_next.start()

    @pl.when(has_prev)
    def _():
        left_prev.start()

    def right_copy(step):
        return send(right_land.at[me], right_land.at[me], right_send.at[step], right_recv.at[me], lax.rem(me + step, n))

    @pl.loop(1, n)
    def _(step):
        right_copy(step).start()

    left_ext[...] = jnp.zeros(left_ext.shape, F32)
    left_ext[8:8 + band, :] = own_left[...].astype(F32)

    @pl.when(has_prev)
    def _():
        left_next.wait_recv()
        left_ext[7:8, :] = left_halo[0].astype(F32)[band - 1:band, :]

    @pl.when(has_next)
    def _():
        left_prev.wait_recv()
        left_ext[8 + band:9 + band, :] = left_halo[1].astype(F32)[0:1, :]

    @pl.loop(1, n)
    def _(step):
        slot = lax.rem(me + step, n)
        send(right_land.at[slot], right_land.at[slot], right_send.at[step], right_recv.at[slot], slot).wait_recv()

    @pl.when(has_next)
    def _():
        to_next.wait_send()
        left_next.wait_send()

    @pl.when(has_prev)
    def _():
        to_prev.wait_send()
        left_prev.wait_send()

    for copy in sent:
        copy.wait_send()

    @pl.loop(1, n)
    def _(step):
        right_copy(step).wait_send()

    track_out.wait()


def pair_kernel(
    track_in, left_ext, right_land, wp_hbm, track_out, pair_out,
    track, wp, right_all, act, pair, w_sem, track_sem, pair_sem,
):
    load = pltpu.make_async_copy(wp_hbm, wp, w_sem)
    load.start()
    track_load = pltpu.make_async_copy(track_in, track, track_sem)
    track_load.start()
    columns, channels = right_all.shape
    band = pair.shape[0]
    right_all[...] = right_land[...].astype(F32).reshape(columns, channels)
    column = lax.broadcasted_iota(jnp.int32, (columns, channels), 0)

    @pl.loop(0, band + 2)
    def _(i):
        product = (left_ext[pl.ds(i + 7, 1), :] * right_all[...]).astype(BF16).astype(F32)
        active = jax.nn.gelu(product)
        act[i, :, 0:channels] = jnp.where(column == 0, 0.0, pltpu.roll(active, 1, 0)).astype(BF16)
        act[i, :, channels:2 * channels] = active.astype(BF16)
        act[i, :, 2 * channels:] = jnp.where(column == columns - 1, 0.0, pltpu.roll(active, columns - 1, 0)).astype(BF16)

    span = 3 * channels
    track_load.wait()
    track_store = pltpu.make_async_copy(track, track_out, track_sem)
    track_store.start()
    load.wait()

    def store(i):
        return pltpu.make_async_copy(pair.at[i], pair_out.at[i], pair_sem.at[i])

    @pl.loop(0, band)
    def _(i):
        total = (left_ext[pl.ds(i + 8, 1), :] * right_all[...]).astype(BF16).astype(F32)
        for a in range(3):
            total = total + dot(act[i + a], wp[a * span:(a + 1) * span, :])
        pair[i] = total.astype(BF16)
        store(i).start()

    track_store.wait()

    @pl.loop(0, band)
    def _(i):
        store(i).wait()


def solution(mesh):
    n = mesh.shape["seq"]

    def local(sequence, gain_conv, conv_weight, gain_attn, w_query, w_key, w_value, w_out, w_left, w_right, w_pair):
        rows, width = sequence.shape
        key, val = w_key.shape[1], w_value.shape[1]
        channels = w_left.shape[1]
        band = rows // POOL
        columns = n * band
        chips = n // 2
        value_lanes = (val // 128 + 1) * 128
        taps = w_pair.reshape(-1, channels)
        weights = (w_query, w_key, w_value.T, w_out, w_left, w_right)
        anyspace = pl.BlockSpec(memory_space=pl.ANY)
        vmem = pl.BlockSpec(memory_space=pltpu.VMEM)
        dma = pltpu.SemaphoreType.DMA
        steps = max(chips // 2, 1)
        track, left, right = pl.pallas_call(
            functools.partial(kernel, n),
            out_shape=(
                jax.ShapeDtypeStruct((rows, width), BF16),
                jax.ShapeDtypeStruct((band + 16, channels), F32),
                jax.ShapeDtypeStruct((n, band, channels), BF16),
            ),
            in_specs=[vmem] * 2 + [anyspace] * 8,
            out_specs=(anyspace, vmem, vmem),
            scratch_shapes=[pltpu.VMEM((2, width), F32)]
            + [pltpu.VMEM(w.shape, BF16) for w in weights]
            + [
                pltpu.VMEM((rows, width), BF16),
                pltpu.VMEM((2, HALO, width), BF16),
                pltpu.VMEM((rows + 2 * HALO, width), F32),
                pltpu.VMEM((rows, width), BF16),
                pltpu.VMEM((rows, width), BF16),
                pltpu.VMEM((HEADS, rows, key), BF16),
                pltpu.VMEM((n, rows, key + value_lanes), BF16),
                pltpu.VMEM((HEADS, rows, value_lanes), F32),
                pltpu.VMEM((HEADS, rows, 128), F32),
                pltpu.VMEM((rows, HEADS * val), BF16),
                pltpu.VMEM((band, channels), BF16),
                pltpu.VMEM((2, band, channels), BF16),
                dma((len(weights) + 2,)),
                dma(()),
                dma((2,)),
                dma((2,)),
                dma((steps, PARTS)),
                dma((steps, PARTS)),
                dma((chips, PARTS)),
                dma((n, PARTS)),
                dma((2,)),
                dma((2,)),
                dma((n,)),
                dma((n,)),
            ],
            compiler_params=pltpu.CompilerParams(
                collective_id=0, has_side_effects=True, vmem_limit_bytes=60 * 1024 * 1024
            ),
        )(sequence, conv_weight, gain_conv, gain_attn, *weights)
        return pl.pallas_call(
            pair_kernel,
            out_shape=(
                jax.ShapeDtypeStruct((rows, width), BF16),
                jax.ShapeDtypeStruct((band, columns, channels), BF16),
            ),
            in_specs=[anyspace, vmem, vmem, anyspace],
            out_specs=(anyspace, anyspace),
            scratch_shapes=[
                pltpu.VMEM((rows, width), BF16),
                pltpu.VMEM(taps.shape, BF16),
                pltpu.VMEM((columns, channels), F32),
                pltpu.VMEM((band + 2, columns, 3 * channels), BF16),
                pltpu.VMEM((band, columns, channels), BF16),
                dma(()),
                dma(()),
                dma((band,)),
            ],
            compiler_params=pltpu.CompilerParams(vmem_limit_bytes=60 * 1024 * 1024),
        )(track, left, right, taps)

    placed = (P(("groups", "seq"), None),) + (P(),) * 10
    return jax.shard_map(
        local,
        mesh=mesh,
        in_specs=placed,
        out_specs=(P(("groups", "seq"), None), P(("groups", "seq"), None, None)),
        check_vma=False,
    )
```

```python
import functools
import math

import jax
import jax.numpy as jnp
from jax import lax
from jax.experimental import pallas as pl
from jax.experimental.pallas import tpu as pltpu
from jax.sharding import PartitionSpec as P

HEADS = 8
POOL = 16
HALO = 16
PARTS = 2
F32 = jnp.float32
BF16 = jnp.bfloat16


def dot(a, b):
    return jnp.dot(a, b, preferred_element_type=F32)


def dot_t(a, b):
    return lax.dot_general(a, b, (((1,), (1,)), ((), ())), preferred_element_type=F32)


def rms_norm(values, gain):
    scale = lax.rsqrt(jnp.mean(values * values, axis=-1, keepdims=True) + 1e-06)
    return values * scale * gain


def kernel(
    n,
    seq_ref, conv_ref,
    gconv_hbm, gattn_hbm, wq_hbm, wk_hbm, wv_hbm, wo_hbm, wl_hbm, wr_hbm,
    track_hbm, left_ext, right_land,
    gains, wq, wk, wv, wo, wl, wr, track_ref,
    halo, padded, first, attn, q_ref, kv, acc, top, attended,
    own_left, left_halo, turned, stage,
    w_sem, track_sem, halo_send, halo_recv, r_send, l_send, p_send, kv_recv,
    left_send, left_recv, right_send, right_recv,
):
    rows, width = seq_ref.shape
    key = wk.shape[1]
    val = wv.shape[0]
    taps = conv_ref.shape[0]
    reach = taps // 2
    part = rows // PARTS
    chips = n // 2
    half = (chips + 1) // 2
    me = lax.axis_index("seq")
    chip = me // 2
    core = me % 2
    partner = chip * 2 + (1 - core)
    pos = jnp.where(chip % 2 == 0, chip // 2, chips - 1 - chip // 2)

    def chip_at(place):
        place = lax.rem(place + 2 * chips, chips)
        return jnp.where(place < half, 2 * place, 2 * (chips - 1 - place) + 1)

    def mine_at(place):
        return chip_at(place) * 2 + core

    def other_at(place):
        return chip_at(place) * 2 + (1 - core)

    barrier = pltpu.get_barrier_semaphore()

    @pl.loop(1, n)
    def _(step):
        pl.semaphore_signal(barrier, inc=1, device_id={"seq": lax.rem(me + step, n)})

    pairs = (
        (wk_hbm, wk), (wv_hbm, wv), (wq_hbm, wq), (wo_hbm, wo), (wl_hbm, wl), (wr_hbm, wr),
        (gconv_hbm, gains.at[0]), (gattn_hbm, gains.at[1]),
    )
    loads = [pltpu.make_async_copy(s, d, w_sem.at[i]) for i, (s, d) in enumerate(pairs)]
    for load in loads[6:] + loads[:6]:
        load.start()

    def send(src, dst, ssem, rsem, to):
        return pltpu.make_async_remote_copy(
            src_ref=src, dst_ref=dst, send_sem=ssem, recv_sem=rsem, device_id={"seq": to}
        )

    has_prev = me > 0
    has_next = me < n - 1
    prev = lax.rem(me + n - 1, n)
    after = lax.rem(me + 1, n)
    to_next = send(seq_ref.at[pl.ds(rows - HALO, HALO)], halo.at[0], halo_send.at[0], halo_recv.at[0], after)
    to_prev = send(seq_ref.at[pl.ds(0, HALO)], halo.at[1], halo_send.at[1], halo_recv.at[1], prev)

    loads[6].wait()
    loads[7].wait()
    gconv = gains[0:1, :]
    strip = 32
    for start in range(0, rows, strip):
        values = seq_ref[start:start + strip, :].astype(F32)
        padded[HALO + start:HALO + start + strip, :] = rms_norm(values, gconv).astype(BF16).astype(F32)

    pl.semaphore_wait(barrier, n - 1)

    @pl.when(has_next)
    def _():
        to_next.start()

    @pl.when(has_prev)
    def _():
        to_prev.start()

    gattn = gains[1:2, :]
    def mix(start):
        total = seq_ref[start:start + strip, :].astype(F32)
        conv = jnp.zeros((strip, width), F32)
        for tap in range(taps):
            base = HALO + start + tap - reach
            conv = conv + conv_ref[tap:tap + 1, :] * padded[base:base + strip, :]
        one = (total + conv).astype(BF16)
        first[start:start + strip, :] = one
        attn[start:start + strip, :] = rms_norm(one.astype(F32), gattn).astype(BF16)

    for start in range(strip, rows - strip, strip):
        mix(start)

    @pl.when(has_prev)
    def _():
        to_next.wait_recv()
        padded[0:HALO, :] = rms_norm(halo[0].astype(F32), gconv).astype(BF16).astype(F32)

    @pl.when(jnp.logical_not(has_prev))
    def _():
        padded[0:HALO, :] = jnp.zeros((HALO, width), F32)

    @pl.when(has_next)
    def _():
        to_prev.wait_recv()
        padded[HALO + rows:, :] = rms_norm(halo[1].astype(F32), gconv).astype(BF16).astype(F32)

    @pl.when(jnp.logical_not(has_next))
    def _():
        padded[HALO + rows:, :] = jnp.zeros((HALO, width), F32)

    mix(0)
    if rows > strip:
        mix(rows - strip)

    loads[0].wait()
    loads[1].wait()
    kv[me, :, 0:key] = dot(attn[...], wk[...]).astype(BF16)
    kv[me, :, key:key + val] = dot_t(attn[...], wv[...]).astype(BF16)
    kv[me, :, key + val:] = jnp.ones((rows, kv.shape[2] - key - val), BF16)

    right_steps = chips // 2
    left_steps = chips - 1 - right_steps
    to_right = mine_at(pos + 1)
    to_left = mine_at(pos - 1)

    def piece(slot, c):
        return kv.at[slot, pl.ds(c * part, part)]

    def copy_right(t, c):
        slot = mine_at(pos - t)
        return send(piece(slot, c), piece(slot, c), r_send.at[t, c], kv_recv.at[slot, c], to_right)

    def copy_left(t, c):
        slot = mine_at(pos + t)
        return send(piece(slot, c), piece(slot, c), l_send.at[t, c], kv_recv.at[slot, c], to_left)

    def copy_partner(slot, count, c):
        return send(piece(slot, c), piece(slot, c), p_send.at[count, c], kv_recv.at[slot, c], partner)

    def arrived(slot, c):
        send(piece(slot, c), piece(slot, c), p_send.at[0, c], kv_recv.at[slot, c], partner).wait_recv()

    sent = []

    def go(copy):
        copy.start()
        sent.append(copy)

    for c in range(PARTS):
        if right_steps:
            go(copy_right(0, c))
        if left_steps:
            go(copy_left(0, c))
        go(copy_partner(me, 0, c))

    loads[2].wait()
    scale = math.log2(math.e) / math.sqrt(key)
    for h in range(HEADS):
        q_ref[h] = (dot(attn[...], wq[:, h * key:(h + 1) * key]) * scale).astype(BF16)

    def attend(pieces, initial):
        keys = jnp.concatenate([kv[s, c * part:(c + 1) * part, 0:key] for s, c in pieces], axis=0)
        count = keys.shape[0]
        wide = count // 128
        turned[:, 0:count] = keys.T
        for k, (s, c) in enumerate(pieces):
            stage[k * part:(k + 1) * part, :] = kv[s, c * part:(c + 1) * part, key:]

        @pl.loop(0, HEADS, unroll=4)
        def _(h):
            scores = dot(q_ref[h], turned[:, 0:count])
            best = jnp.broadcast_to(jnp.max(scores, axis=1, keepdims=True), (rows, 128))
            if not initial:
                old = top[h]
                best = jnp.maximum(old, best)
            weights = jnp.exp2((scores - jnp.concatenate([best] * wide, axis=1)).astype(BF16))
            update = dot(weights, stage[0:count, :])
            if initial:
                acc[h] = update
            else:
                factor = jnp.exp2(old - best)
                acc[h] = acc[h] * jnp.concatenate([factor] * (update.shape[1] // 128), axis=1) + update
            top[h] = best

    for c in range(PARTS):
        arrived(partner, c)
    attend([(s, c) for s in (me, partner) for c in range(PARTS)], True)

    waiting = None
    count = 1
    for t in range(right_steps):
        both = t < left_steps
        slots = [pos - 1 - t] + ([pos + 1 + t] if both else [])
        for c in range(PARTS):
            for k, place in enumerate(slots):
                slot = mine_at(place)
                arrived(slot, c)
                if k == 0 and t + 1 < right_steps:
                    go(copy_right(t + 1, c))
                if k == 1 and t + 1 < left_steps:
                    go(copy_left(t + 1, c))
                go(copy_partner(slot, count + k, c))
            if waiting is not None:
                for s, cc in waiting[1]:
                    arrived(s, cc)
                attend(waiting[0] + waiting[1], False)
            waiting = ([(mine_at(p), c) for p in slots], [(other_at(p), c) for p in slots])
        count += len(slots)
    if waiting is not None:
        for s, cc in waiting[1]:
            arrived(s, cc)
        attend(waiting[0] + waiting[1], False)

    for pair in range(0, HEADS, 2):
        both = []
        for h in (pair, pair + 1):
            block = acc[h]
            both.append((block[:, :val] * (1.0 / block[:, val:val + 1])).astype(BF16))
        attended[:, pair * val:(pair + 2) * val] = jnp.concatenate(both, axis=1)

    loads[3].wait()
    band = rows // POOL
    member = lax.broadcasted_iota(jnp.int32, (band, rows), 1) // POOL
    pool = jnp.where(member == lax.broadcasted_iota(jnp.int32, (band, rows), 0), 1.0 / POOL, 0.0).astype(BF16)
    loads[4].wait()
    loads[5].wait()
    left = jnp.zeros((band, wl.shape[1]), F32)
    right = jnp.zeros((band, wr.shape[1]), F32)
    cols = 512 if width % 512 == 0 else width
    for start in range(0, width, cols):
        stop = start + cols
        block = (first[:, start:stop].astype(F32) + dot(attended[...], wo[:, start:stop])).astype(BF16)
        track_ref[:, start:stop] = block
        pooled = dot(pool, block).astype(BF16)
        left = left + dot(pooled, wl[start:stop, :])
        right = right + dot(pooled, wr[start:stop, :])
    track_out = pltpu.make_async_copy(track_ref, track_hbm, track_sem)
    track_out.start()
    own_left[...] = left.astype(BF16)
    right_land[me] = right.astype(BF16)

    left_next = send(own_left, left_halo.at[0], left_send.at[0], left_recv.at[0], after)
    left_prev = send(own_left, left_halo.at[1], left_send.at[1], left_recv.at[1], prev)

    @pl.when(has_next)
    def _():
        left_next.start()

    @pl.when(has_prev)
    def _():
        left_prev.start()

    def right_copy(step):
        return send(right_land.at[me], right_land.at[me], right_send.at[step], right_recv.at[me], lax.rem(me + step, n))

    @pl.loop(1, n)
    def _(step):
        right_copy(step).start()

    left_ext[...] = jnp.zeros(left_ext.shape, F32)
    left_ext[8:8 + band, :] = own_left[...].astype(F32)

    @pl.when(has_prev)
    def _():
        left_next.wait_recv()
        left_ext[7:8, :] = left_halo[0].astype(F32)[band - 1:band, :]

    @pl.when(has_next)
    def _():
        left_prev.wait_recv()
        left_ext[8 + band:9 + band, :] = left_halo[1].astype(F32)[0:1, :]

    @pl.loop(1, n)
    def _(step):
        slot = lax.rem(me + step, n)
        send(right_land.at[slot], right_land.at[slot], right_send.at[step], right_recv.at[slot], slot).wait_recv()

    @pl.when(has_next)
    def _():
        to_next.wait_send()
        left_next.wait_send()

    @pl.when(has_prev)
    def _():
        to_prev.wait_send()
        left_prev.wait_send()

    for copy in sent:
        copy.wait_send()

    @pl.loop(1, n)
    def _(step):
        right_copy(step).wait_send()

    track_out.wait()


def pair_kernel(
    track_in, left_ext, right_land, wp_hbm, track_out, pair_out,
    track, wp, right_all, act, pair, w_sem, track_sem, pair_sem,
):
    load = pltpu.make_async_copy(wp_hbm, wp, w_sem)
    load.start()
    track_load = pltpu.make_async_copy(track_in, track, track_sem)
    track_load.start()
    columns, channels = right_all.shape
    band = pair.shape[0]
    right_all[...] = right_land[...].astype(F32).reshape(columns, channels)
    column = lax.broadcasted_iota(jnp.int32, (columns, channels), 0)

    @pl.loop(0, band + 2)
    def _(i):
        product = (left_ext[pl.ds(i + 7, 1), :] * right_all[...]).astype(BF16).astype(F32)
        active = jax.nn.gelu(product)
        act[i, :, 0:channels] = jnp.where(column == 0, 0.0, pltpu.roll(active, 1, 0)).astype(BF16)
        act[i, :, channels:2 * channels] = active.astype(BF16)
        act[i, :, 2 * channels:] = jnp.where(column == columns - 1, 0.0, pltpu.roll(active, columns - 1, 0)).astype(BF16)

    span = 3 * channels
    track_load.wait()
    track_store = pltpu.make_async_copy(track, track_out, track_sem)
    track_store.start()
    load.wait()

    def store(i):
        return pltpu.make_async_copy(pair.at[i], pair_out.at[i], pair_sem.at[i])

    @pl.loop(0, band)
    def _(i):
        total = (left_ext[pl.ds(i + 8, 1), :] * right_all[...]).astype(BF16).astype(F32)
        for a in range(3):
            total = total + dot(act[i + a], wp[a * span:(a + 1) * span, :])
        pair[i] = total.astype(BF16)
        store(i).start()

    track_store.wait()

    @pl.loop(0, band)
    def _(i):
        store(i).wait()


def solution(mesh):
    n = mesh.shape["seq"]

    def local(sequence, gain_conv, conv_weight, gain_attn, w_query, w_key, w_value, w_out, w_left, w_right, w_pair):
        rows, width = sequence.shape
        key, val = w_key.shape[1], w_value.shape[1]
        channels = w_left.shape[1]
        band = rows // POOL
        columns = n * band
        chips = n // 2
        value_lanes = (val // 128 + 1) * 128
        taps = w_pair.reshape(-1, channels)
        weights = (w_query, w_key, w_value.T, w_out, w_left, w_right)
        anyspace = pl.BlockSpec(memory_space=pl.ANY)
        vmem = pl.BlockSpec(memory_space=pltpu.VMEM)
        dma = pltpu.SemaphoreType.DMA
        steps = max(chips // 2, 1)
        track, left, right = pl.pallas_call(
            functools.partial(kernel, n),
            out_shape=(
                jax.ShapeDtypeStruct((rows, width), BF16),
                jax.ShapeDtypeStruct((band + 16, channels), F32),
                jax.ShapeDtypeStruct((n, band, channels), BF16),
            ),
            in_specs=[vmem] * 2 + [anyspace] * 8,
            out_specs=(anyspace, vmem, vmem),
            scratch_shapes=[pltpu.VMEM((2, width), F32)]
            + [pltpu.VMEM(w.shape, BF16) for w in weights]
            + [
                pltpu.VMEM((rows, width), BF16),
                pltpu.VMEM((2, HALO, width), BF16),
                pltpu.VMEM((rows + 2 * HALO, width), F32),
                pltpu.VMEM((rows, width), BF16),
                pltpu.VMEM((rows, width), BF16),
                pltpu.VMEM((HEADS, rows, key), BF16),
                pltpu.VMEM((n, rows, key + value_lanes), BF16),
                pltpu.VMEM((HEADS, rows, value_lanes), F32),
                pltpu.VMEM((HEADS, rows, 128), F32),
                pltpu.VMEM((rows, HEADS * val), BF16),
                pltpu.VMEM((band, channels), BF16),
                pltpu.VMEM((2, band, channels), BF16),
                pltpu.VMEM((key, max(4 * rows // PARTS, 2 * rows)), BF16),
                pltpu.VMEM((max(4 * rows // PARTS, 2 * rows), value_lanes), BF16),
                dma((len(weights) + 2,)),
                dma(()),
                dma((2,)),
                dma((2,)),
                dma((steps, PARTS)),
                dma((steps, PARTS)),
                dma((chips, PARTS)),
                dma((n, PARTS)),
                dma((2,)),
                dma((2,)),
                dma((n,)),
                dma((n,)),
            ],
            compiler_params=pltpu.CompilerParams(
                collective_id=0, has_side_effects=True, vmem_limit_bytes=60 * 1024 * 1024
            ),
        )(sequence, conv_weight, gain_conv, gain_attn, *weights)
        return pl.pallas_call(
            pair_kernel,
            out_shape=(
                jax.ShapeDtypeStruct((rows, width), BF16),
                jax.ShapeDtypeStruct((band, columns, channels), BF16),
            ),
            in_specs=[anyspace, vmem, vmem, anyspace],
            out_specs=(anyspace, anyspace),
            scratch_shapes=[
                pltpu.VMEM((rows, width), BF16),
                pltpu.VMEM(taps.shape, BF16),
                pltpu.VMEM((columns, channels), F32),
                pltpu.VMEM((band + 2, columns, 3 * channels), BF16),
                pltpu.VMEM((band, columns, channels), BF16),
                dma(()),
                dma(()),
                dma((band,)),
            ],
            compiler_params=pltpu.CompilerParams(vmem_limit_bytes=60 * 1024 * 1024),
        )(track, left, right, taps)

    placed = (P(("groups", "seq"), None),) + (P(),) * 10
    return jax.shard_map(
        local,
        mesh=mesh,
        in_specs=placed,
        out_specs=(P(("groups", "seq"), None), P(("groups", "seq"), None, None)),
        check_vma=False,
    )
```
